256 devices in a mesh: seq: 32 (over z, y_lo, core), fsdp: 8 (over x, y_hi).
Axes of the slice: x: 4, y: 4 (y_hi: 2, y_lo: 2; y = y_hi * 2 + y_lo), z: 8, core: 2. Of those that a mesh axis runs over, the one named last changes fastest.
Arguments:
- inputs: bfloat16 [16, 4096, 1536], P('fsdp', 'seq'), may hold values from -6 to 6
- gain: float32 [1536], replicated, may hold values from 0.1 to 1.9
- param: bfloat16 [1536, 3, 1536], P('fsdp'), may hold values from -6 to 6
- cotangent: bfloat16 [16, 4096, 1536], P('fsdp', 'seq'), may hold values from -12 to 12
- noise: bfloat16 [1536, 3, 1536], P('fsdp'), may hold values from -6 to 6
Outputs:
- outputs: bfloat16 [16, 4096, 1536], P('fsdp', 'seq')
- new_param: bfloat16 [1536, 3, 1536], P('fsdp')
The draws below stay inside these ranges and needn't reach their ends.
All inputs are finite; a program needn't handle non-finite values.
Results may differ from the reference program's by a relative error of at most 0.012.
Values may be sent and summed in bfloat16 or wider, within the bound.
No kernel may reach another device: no remote copies, remote signals or barrier semaphores. Data moves between devices by JAX's collectives and lax.ppermute only.
A program may use at most 128 MiB of HBM per device.

```python
import math
import jax
import jax.numpy as jnp
from jax import lax

CHANNEL_COUNT = 1536
SEQUENCE_LENGTH = 4096
DILATION_STEP = 16
SEQUENCES_SHARD = 2
BATCH = 16
POSITIONS_SHARD = 128
N_SEQ = 32
N_FSDP = 8


def draw_cotangent(key, part):
    key = jax.random.fold_in(key, 7)
    value_key = jax.random.fold_in(key, 0)
    pair_key = jax.random.fold_in(key, 2)
    shape = (BATCH, SEQUENCE_LENGTH, CHANNEL_COUNT)
    values = jax.random.truncated_normal(value_key, -3.0, 3.0, shape, jnp.float32)
    block_count = BATCH // SEQUENCES_SHARD
    pairing = jax.random.permutation(pair_key, block_count)
    batch_block = jnp.arange(BATCH) // SEQUENCES_SHARD
    channel_block = jnp.arange(CHANNEL_COUNT) // (CHANNEL_COUNT // block_count)
    chosen = pairing[batch_block][:, None] == channel_block[None, :]
    factor = jnp.where(chosen, 3.0, 1.0).astype(jnp.float32)
    return (values * factor[:, None, :]).astype(jnp.bfloat16)


def block_levels(stream_key, shape, pieces, smallest, high):
    loudness, own = 1.0, jax.random.fold_in(stream_key, 6)
    for axis_at, blocks in pieces:
        heights = jnp.exp(jax.random.uniform(jax.random.fold_in(own, axis_at), (blocks,), jnp.float32, smallest / len(pieces), high / len(pieces)))
        loudness = loudness * jnp.repeat(heights, shape[axis_at] // blocks).reshape([-1 if axis == axis_at else 1 for axis in range(len(shape))])
    return loudness


def centred(stream_key, dims, spread, limit, cuts=(), kind=jnp.bfloat16):
    result = jax.random.normal(stream_key, dims, jnp.float32) * spread
    if len(cuts) > 0:
        result = block_levels(stream_key, dims, cuts, -0.22, 0.18) * result
    return jnp.clip(result, min=-limit, max=limit).astype(kind)


def setup_inputs(seed: int = 0) -> dict:
    splits = jax.random.split(jax.random.key(seed), 6)
    return {
        "inputs": centred(splits[0], (BATCH, SEQUENCE_LENGTH, CHANNEL_COUNT), 1.0, 6.0, ((0, 8), (1, 32))),
        "gain": jnp.clip(1.0 + 0.18 * jax.random.normal(splits[1], (CHANNEL_COUNT,), jnp.float32), 0.1, 1.9),
        "param": centred(splits[2], (CHANNEL_COUNT, 3, CHANNEL_COUNT), 1.0, 6.0, ((0, 8),)),
        "cotangent": draw_cotangent(jax.random.fold_in(splits[5], 71), 0),
        "noise": centred(splits[4], (CHANNEL_COUNT, 3, CHANNEL_COUNT), 1.0, 6.0, ((0, 8),)),
    }


def normalise(values, gain):
    floats = values.astype(jnp.float32)
    factor = lax.rsqrt(lax.optimization_barrier(jnp.mean(floats * floats, axis=-1, keepdims=True)) + 1e-06)
    return jax.nn.gelu(floats * factor * gain).astype(jnp.bfloat16)

def reference(inputs, gain, param, cotangent, noise):
    scale = 1.0 / math.sqrt(3.0 * CHANNEL_COUNT)
    hidden_state = normalise(inputs, gain)
    padded_input = jnp.pad(hidden_state, ((0, 0), (DILATION_STEP, DILATION_STEP), (0, 0)))

    def forward_one(sequence_index):
        total = jnp.zeros((SEQUENCE_LENGTH, CHANNEL_COUNT), jnp.float32)
        for kernel_tap in range(3):
            input_window = sequence_index[kernel_tap * DILATION_STEP:kernel_tap * DILATION_STEP + SEQUENCE_LENGTH, :]
            total = total + jnp.dot(input_window, param[:, kernel_tap, :].T, preferred_element_type=jnp.float32)
        return total * scale
    mixed = lax.map(forward_one, padded_input)
    outputs = (inputs.astype(jnp.float32) + mixed).astype(jnp.bfloat16)
    zeroed_index = jnp.zeros((), jnp.int32)

    def add_block(index, total):
        index = jnp.asarray(index).astype(jnp.int32)
        row_tile = index // N_SEQ
        position_block = index % N_SEQ
        hidden_tile = lax.dynamic_slice(padded_input, (row_tile * SEQUENCES_SHARD, position_block * POSITIONS_SHARD, zeroed_index), (SEQUENCES_SHARD, POSITIONS_SHARD + 2 * DILATION_STEP, CHANNEL_COUNT))
        grad_block = lax.dynamic_slice(cotangent, (row_tile * SEQUENCES_SHARD, position_block * POSITIONS_SHARD, zeroed_index), (SEQUENCES_SHARD, POSITIONS_SHARD, CHANNEL_COUNT))
        flat_grad = grad_block.reshape(SEQUENCES_SHARD * POSITIONS_SHARD, CHANNEL_COUNT)
        taps = []
        for kernel_tap in range(3):
            input_window = hidden_tile[:, kernel_tap * DILATION_STEP:kernel_tap * DILATION_STEP + POSITIONS_SHARD, :].reshape(SEQUENCES_SHARD * POSITIONS_SHARD, CHANNEL_COUNT)
            taps.append(jnp.dot(flat_grad.T, input_window, preferred_element_type=jnp.float32))
        term = (jnp.stack(taps, axis=1) * scale).astype(jnp.bfloat16)
        term = lax.optimization_barrier(term)
        return total + term.astype(jnp.float32)
    grad = lax.fori_loop(0, N_FSDP * N_SEQ, add_block, jnp.zeros((CHANNEL_COUNT, 3, CHANNEL_COUNT), jnp.float32))
    eta = math.sqrt(3.0 * CHANNEL_COUNT / (BATCH * SEQUENCE_LENGTH))
    updated = param.astype(jnp.float32) - eta * grad + math.sqrt(2.0 * eta) * noise.astype(jnp.float32)
    return (outputs, updated.astype(jnp.bfloat16))
```

```python
import math

import jax
import jax.numpy as jnp
from jax import lax
from jax.sharding import Mesh, PartitionSpec as P

D = 16
CHUNKS = 3
F32, BF16 = jnp.float32, jnp.bfloat16


def normalise(values, gain):
    floats = values.astype(F32)
    factor = lax.rsqrt(jnp.mean(floats * floats, axis=-1, keepdims=True) + 1e-06)
    return jax.nn.gelu(floats * factor * gain).astype(BF16)


def ring(axis, step):
    n = lax.axis_size(axis)
    return [(i, (i + step) % n) for i in range(n)]


def seq_shift(step):
    n = lax.axis_size(("z", "ylo", "core"))
    return [(i, i + step) for i in range(n) if 0 <= i + step < n]


SEQ = ("z", "ylo", "core")
OTHER_HALF = [(0, 3), (3, 0), (1, 2), (2, 1)]


def from_x(blocks_to):
    return [blocks_to[0]] + [lax.ppermute(blocks_to[d], "x", ring("x", d)) for d in range(1, 4)]


def gather_x(block):
    left = lax.ppermute(block, "x", ring("x", 1))
    right = lax.ppermute(block, "x", ring("x", -1))
    far0 = lax.ppermute(left[:1], "x", ring("x", 1))
    far1 = lax.ppermute(right[1:], "x", ring("x", -1))
    return jnp.concatenate([block, left, far0, far1, right], axis=0)


def shards(inputs, gain, param, cotangent, noise):
    seqs, span, width = inputs.shape
    rows = param.shape[0]
    scale = 1.0 / math.sqrt(3.0 * width)
    total_rows = seqs * span * 256
    eta = math.sqrt(3.0 * width / total_rows)
    core, ylo, yhi = (lax.axis_index(a) for a in ("core", "ylo", "yhi"))
    x, z = lax.axis_index("x"), lax.axis_index("z")
    outs = 2 * rows
    cw = width // CHUNKS
    half = cw // 2
    quarter = half // 2

    slices = [
        lax.dynamic_slice_in_dim(cotangent, lax.rem(x + d, 4) * outs, outs, 2) for d in range(4)
    ]
    cot = jnp.concatenate(from_x(slices), axis=0)
    before = lax.ppermute(cot[:, span - D :], SEQ, seq_shift(1))
    after = lax.ppermute(cot[:, :D], SEQ, seq_shift(-1))
    cot = jnp.concatenate([before, cot, after], axis=1)
    cots = jnp.concatenate([cot[:, (2 - k) * D : (2 - k) * D + span] for k in range(3)], axis=2)

    kernel = jnp.transpose(param, (1, 0, 2))
    part = lax.dynamic_slice_in_dim(kernel, core * (width // 2), width // 2, 2)
    part = lax.ppermute(part, ("ylo", "yhi"), OTHER_HALF)
    mate = lax.ppermute(part, "core", ring("core", 1))
    low = jnp.where(core == 0, part, mate)
    high = jnp.where(core == 0, mate, part)
    other = jnp.concatenate([low, high], axis=2)

    hidden = normalise(inputs, gain)
    old = kernel.reshape(3 * rows, width)
    fresh = jnp.transpose(noise, (1, 0, 2)).reshape(3 * rows, width)
    piece = 3 * rows // 8

    gathered, news = [], []
    for c in range(CHUNKS):
        block = gather_x(hidden[:, :, c * cw : (c + 1) * cw])
        gathered.append(block)
        grad = lax.dot_general(
            cots, block, (((0, 1), (0, 1)), ((), ())), preferred_element_type=F32
        ) * scale
        keep = lax.dynamic_slice_in_dim(grad, core * half, half, 1)
        send = lax.dynamic_slice_in_dim(grad, (1 - core) * half, half, 1).astype(BF16)
        got = lax.ppermute(send, "core", ring("core", 1))
        both = (keep + got.astype(F32)).astype(BF16)
        both = both.reshape(3, 2, rows, 2, quarter)
        both = jnp.transpose(both, (3, 1, 0, 2, 4)).reshape(4, 3 * rows, quarter)
        terms = lax.all_to_all(both, ("ylo", "yhi"), 0, 0, tiled=True)
        summed = jnp.sum(terms.astype(F32), axis=0).astype(BF16)
        terms = lax.all_to_all(summed.reshape(8, piece, quarter), "z", 0, 0, tiled=True)
        summed = jnp.sum(terms.astype(F32), axis=0)
        at = (z * piece, c * cw + core * half + ylo * quarter)
        own_param = lax.dynamic_slice(old, at, (piece, quarter))
        own_noise = lax.dynamic_slice(fresh, at, (piece, quarter))
        new = (
            own_param.astype(F32) - eta * summed + math.sqrt(2.0 * eta) * own_noise.astype(F32)
        ).astype(BF16)
        new = jnp.broadcast_to(new[None], (16, piece, quarter))
        new = lax.all_to_all(new, ("z", "ylo"), 0, 0, tiled=True)
        new = jnp.transpose(new.reshape(8, 2, piece, quarter), (0, 2, 1, 3)).reshape(3 * rows, half)
        mine = new
        mate = lax.ppermute(new, "core", ring("core", 1))
        news += [jnp.where(core == 0, mine, mate), jnp.where(core == 0, mate, mine)]
    new_param = jnp.concatenate(news, axis=1).reshape(3, rows, width)
    new_param = jnp.transpose(new_param, (1, 0, 2))

    hid = jnp.concatenate(gathered, axis=2)
    both = [
        lax.dot_general(hid, w, (((2,), (2,)), ((), ())), preferred_element_type=F32)
        for w in (jnp.where(yhi == 0, kernel, other), jnp.where(yhi == 0, other, kernel))
    ]
    prods = jnp.concatenate(both, axis=3)
    from_before = lax.ppermute(prods[:, span - D :, 0].astype(BF16), SEQ, seq_shift(1)).astype(F32)
    from_after = lax.ppermute(prods[:, :D, 2].astype(BF16), SEQ, seq_shift(-1)).astype(F32)
    mixed = (
        prods[:, :, 1]
        + jnp.concatenate([from_before, prods[:, : span - D, 0]], axis=1)
        + jnp.concatenate([prods[:, D:, 2], from_after], axis=1)
    ) * scale
    mixed = mixed.astype(BF16).reshape(4, seqs, span, outs)
    back = [mixed[0]] + [lax.ppermute(mixed[d], "x", ring("x", -d)) for d in range(1, 4)]
    total = jnp.zeros((seqs, span, width), BF16)
    for d in range(4):
        total = lax.dynamic_update_slice_in_dim(total, back[d], lax.rem(x + d, 4) * outs, 2)
    outputs = (inputs.astype(F32) + total.astype(F32)).astype(BF16)
    return (outputs, new_param)


def solution(mesh):
    fine = Mesh(mesh.devices.reshape(8, 2, 2, 4, 2), ("z", "ylo", "core", "x", "yhi"))
    spread = P(("x", "yhi"), SEQ, None)
    placed = (spread, P(), P(("x", "yhi"), None, None), spread, P(("x", "yhi"), None, None))
    return jax.shard_map(
        shards,
        mesh=fine,
        in_specs=placed,
        out_specs=(spread, P(("x", "yhi"), None, None)),
        check_vma=False,
    )
```

```python
import math

import jax
import jax.numpy as jnp
from jax import lax
from jax.sharding import Mesh, PartitionSpec as P

D = 16
F32, BF16 = jnp.float32, jnp.bfloat16
SEQ = ("z", "ylo", "core")
PLANE = ("ylo", "core", "x", "yhi")
SIZES = (2, 2, 4, 2)


def plane_perm(move):
    pairs = []
    for ylo in range(2):
        for core in range(2):
            for x in range(4):
                for yhi in range(2):
                    tx, ty = (v % 4 for v in move(core, x, 2 * yhi + ylo))
                    source = ((ylo * 2 + core) * 4 + x) * 2 + yhi
                    target = (((ty % 2) * 2 + core) * 4 + tx) * 2 + ty // 2
                    pairs.append((source, target))
    return pairs


def along(step):
    return plane_perm(lambda c, x, y: (x + step, y) if c == 0 else (x, y + step))


def across(step):
    return plane_perm(lambda c, x, y: (x, y + step) if c == 0 else (x + step, y))


def outward():
    n = lax.axis_size(SEQ)
    pairs = []
    for i in range(n):
        j = i - 1 if i % 2 == 0 else i + 1
        if 0 <= j < n:
            pairs.append((i, j))
    return pairs


def swap(v):
    return lax.ppermute(v, "core", [(0, 1), (1, 0)])


def normalise(values, gain):
    floats = values.astype(F32)
    factor = lax.rsqrt(jnp.mean(floats * floats, axis=-1, keepdims=True) + 1e-06)
    return jax.nn.gelu(floats * factor * gain).astype(BF16)


def shards(inputs, gain, param, cotangent, noise):
    seqs, span, width = inputs.shape
    rows = param.shape[0]
    outs = 2 * rows
    half = width // 2
    scale = 1.0 / math.sqrt(3.0 * width)
    total_rows = seqs * span * 256
    eta = math.sqrt(3.0 * width / total_rows)
    core, ylo, yhi, x, z = (lax.axis_index(a) for a in ("core", "ylo", "yhi", "x", "z"))
    y = 2 * yhi + ylo
    first = core == 0
    me = jnp.where(first, x, y)
    over = jnp.where(first, y, x)

    edge = jnp.where(first, inputs[:, :D], inputs[:, span - D :])
    edge = lax.ppermute(edge, SEQ, outward())

    mate = swap(cotangent)
    chip = jnp.stack([jnp.where(first, cotangent, mate), jnp.where(first, mate, cotangent)], 1)
    cots = [lax.dynamic_slice_in_dim(chip, lax.rem(me + d, 4) * outs, outs, 3) for d in range(4)]
    cots = [cots[0]] + [lax.ppermute(cots[d], PLANE, along(d)) for d in range(1, 4)]
    cots = [c.reshape(seqs, 2 * span, outs) for c in cots]

    own = normalise(inputs, gain)
    edge = normalise(edge, gain)
    ext = jnp.where(
        first, jnp.concatenate([edge, own], axis=1), jnp.concatenate([own, edge], axis=1)
    )
    low, high = ext[:, :, :half], ext[:, :, half:]
    mine = jnp.where(first, low, high)
    mate = swap(jnp.where(first, high, low))
    block = jnp.concatenate([jnp.where(first, mine, mate), jnp.where(first, mate, mine)], axis=1)

    left = lax.ppermute(block, PLANE, along(1))
    right = lax.ppermute(block, PLANE, along(-1))
    far0 = lax.ppermute(left[:1], PLANE, along(1))
    far1 = lax.ppermute(right[1:], PLANE, along(-1))
    blocks = jnp.concatenate([block, left, far0, far1, right], axis=0)
    cot = jnp.concatenate(cots, axis=0)

    windows = [blocks[:, k * D : k * D + 2 * span] for k in range(3)]
    grad = jnp.stack(
        [
            lax.dot_general(cot, w, (((0, 1), (0, 1)), ((), ())), preferred_element_type=F32)
            for w in windows
        ]
    )
    grad = (grad * scale).astype(BF16)
    quarter = half // 2
    grad = jnp.transpose(grad.reshape(3, 2, rows, 2, quarter), (1, 3, 0, 2, 4))
    grad = grad.reshape(4, 3 * rows, quarter)
    terms = [lax.dynamic_index_in_dim(grad, lax.rem(over + d, 4), 0, False) for d in range(4)]
    terms = [terms[0]] + [lax.ppermute(terms[d], PLANE, across(d)) for d in range(1, 4)]
    summed = sum(t.astype(F32) for t in terms).astype(BF16)
    piece = 3 * rows // 8
    terms = lax.all_to_all(summed.reshape(8, piece, quarter), "z", 0, 0, tiled=True)
    summed = jnp.sum(terms.astype(F32), axis=0).astype(BF16)
    summed = lax.ppermute(
        summed, PLANE, plane_perm(lambda c, x, y: (x, y) if c == 0 else (y, x))
    )
    kernel = jnp.transpose(param, (1, 0, 2))
    at = (z * piece, core * half + ylo * quarter)
    own_param = lax.dynamic_slice(kernel.reshape(3 * rows, width), at, (piece, quarter))
    own_noise = lax.dynamic_slice(
        jnp.transpose(noise, (1, 0, 2)).reshape(3 * rows, width), at, (piece, quarter)
    )
    new = (
        own_param.astype(F32)
        - eta * summed.astype(F32)
        + math.sqrt(2.0 * eta) * own_noise.astype(F32)
    ).astype(BF16)
    new = jnp.broadcast_to(new[None], (16, piece, quarter))
    new = lax.all_to_all(new, ("z", "ylo"), 0, 0, tiled=True)
    new = jnp.transpose(new.reshape(8, 2, piece, quarter), (0, 2, 1, 3)).reshape(3 * rows, half)
    mate = swap(new)
    new = jnp.concatenate([jnp.where(first, new, mate), jnp.where(first, mate, new)], axis=1)
    new_param = jnp.transpose(new.reshape(3, rows, width), (1, 0, 2))

    share = lax.dynamic_slice_in_dim(kernel, core * half, half, 2)
    one = lax.ppermute(share, PLANE, plane_perm(lambda c, x, y: (x, y) if c == 0 else (y, x)))
    two = lax.ppermute(
        share, PLANE, plane_perm(lambda c, x, y: (x, 3 - y) if c == 0 else (y + 2, x))
    )
    order = over < 2
    weights = jnp.concatenate([jnp.where(order, one, two), jnp.where(order, two, one)], axis=1)
    mixed = sum(
        lax.dot_general(w, weights[k], (((2,), (1,)), ((), ())), preferred_element_type=F32)
        for k, w in enumerate(windows)
    )
    mixed = (mixed * scale).astype(BF16).reshape(4, seqs, 2 * span, outs)
    back = [mixed[0]] + [lax.ppermute(mixed[d], PLANE, along(-d)) for d in range(1, 4)]
    total = jnp.zeros((seqs, 2 * span, width), BF16)
    for d in range(4):
        total = lax.dynamic_update_slice_in_dim(total, back[d], lax.rem(me + d, 4) * outs, 2)
    near, away = total[:, :span], total[:, span:]
    mate = swap(jnp.where(first, away, near))
    near = jnp.where(first, near, away)
    outputs = (inputs.astype(F32) + (near.astype(F32) + mate.astype(F32))).astype(BF16)
    return (outputs, new_param)


def solution(mesh):
    fine = Mesh(mesh.devices.reshape(8, 2, 2, 4, 2), ("z", "ylo", "core", "x", "yhi"))
    spread = P(("x", "yhi"), SEQ, None)
    placed = (spread, P(), P(("x", "yhi"), None, None), spread, P(("x", "yhi"), None, None))
    return jax.shard_map(
        shards,
        mesh=fine,
        in_specs=placed,
        out_specs=(spread, P(("x", "yhi"), None, None)),
        check_vma=False,
    )
```

```python
import functools
import math

import jax
import jax.numpy as jnp
from jax import lax
from jax.experimental import pallas as pl
from jax.experimental.pallas import tpu as pltpu
from jax.sharding import Mesh, PartitionSpec as P

D = 16
F32, BF16 = jnp.float32, jnp.bfloat16
SEQ = ("z", "ylo", "core")
PLANE = ("ylo", "core", "x", "yhi")
SIZES = (2, 2, 4, 2)


def plane_perm(move):
    pairs = []
    for ylo in range(2):
        for core in range(2):
            for x in range(4):
                for yhi in range(2):
                    tx, ty = (v % 4 for v in move(core, x, 2 * yhi + ylo))
                    source = ((ylo * 2 + core) * 4 + x) * 2 + yhi
                    target = (((ty % 2) * 2 + core) * 4 + tx) * 2 + ty // 2
                    pairs.append((source, target))
    return pairs


def along(step):
    return plane_perm(lambda c, x, y: (x + step, y) if c == 0 else (x, y + step))


def across(step):
    return plane_perm(lambda c, x, y: (x, y + step) if c == 0 else (x + step, y))


def outward():
    n = lax.axis_size(SEQ)
    pairs = []
    for i in range(n):
        j = i - 1 if i % 2 == 0 else i + 1
        if 0 <= j < n:
            pairs.append((i, j))
    return pairs


def swap(v):
    return lax.ppermute(v, "core", [(0, 1), (1, 0)])


def normalise(values, gain):
    floats = values.astype(F32)
    factor = lax.rsqrt(jnp.mean(floats * floats, axis=-1, keepdims=True) + 1e-06)
    return jax.nn.gelu(floats * factor * gain).astype(BF16)


def in_vmem(count):
    return [pl.BlockSpec(memory_space=pltpu.VMEM)] * count


def call(kernel, shapes, scalars, arrays, flops, scratch=()):
    size = sum(math.prod(a.shape) * a.dtype.itemsize for a in (*arrays, *shapes))
    return pl.pallas_call(
        kernel,
        out_shape=shapes,
        in_specs=[pl.BlockSpec(memory_space=pltpu.SMEM)] * len(scalars) + in_vmem(len(arrays)),
        out_specs=in_vmem(len(shapes)),
        scratch_shapes=list(scratch),
        cost_estimate=pl.CostEstimate(flops=flops, bytes_accessed=size, transcendentals=0),
        compiler_params=pltpu.CompilerParams(vmem_limit_bytes=40 * 2**20),
    )(*scalars, *arrays)


def turn_kernel(*refs):
    for source, target in zip(refs[:4], refs[4:]):
        for b in range(2):
            n = source.shape[1]
            target[:, b * n : (b + 1) * n] = source[b].T


def grad_kernel(scale, over, *refs):
    turned, blocks, out = refs[:4], refs[4:8], refs[8]
    outs = turned[0].shape[0]
    rows, n = outs // 2, turned[0].shape[1] // 2
    width = blocks[0].shape[2]
    quarter, tile = width // 2, 256
    for k in range(3):
        for at in range(0, width, tile):
            total = jnp.zeros((outs, tile), F32)
            for t, block in zip(turned, blocks):
                for b in range(2):
                    total += jnp.dot(
                        t[:, b * n : (b + 1) * n],
                        block[b, k * D : k * D + n, at : at + tile],
                        preferred_element_type=F32,
                    )
            total = (total * scale).astype(BF16)
            for sub in range(2):
                lo, hi = max(at, sub * quarter), min(at + tile, (sub + 1) * quarter)
                if lo >= hi:
                    continue
                for part in range(2):
                    slot = (2 * part + sub - over[0] + 4) & 3
                    out[slot, k * rows : (k + 1) * rows, lo - sub * quarter : hi - sub * quarter] = (
                        total[part * rows : (part + 1) * rows, lo - at : hi - at]
                    )


def mixed_kernel(scale, over, one, two, *refs):
    blocks, results, weights = refs[:4], refs[4:8], refs[8]
    rows, n = one.shape[1], results[0].shape[1]
    swapped = jnp.where(over[0] < 2, 0, rows)
    for k in range(3):
        weights[k, pl.ds(pl.multiple_of(swapped, rows), rows), :] = one[k]
        weights[k, pl.ds(pl.multiple_of(rows - swapped, rows), rows), :] = two[k]
    for block, result in zip(blocks, results):
        for b in range(2):
            total = jnp.zeros((n, 2 * rows), F32)
            for k in range(3):
                total += lax.dot_general(
                    block[b, k * D : k * D + n],
                    weights[k],
                    (((1,), (1,)), ((), ())),
                    preferred_element_type=F32,
                )
            result[b] = (total * scale).astype(BF16)


def shards(inputs, gain, param, cotangent, noise):
    seqs, span, width = inputs.shape
    rows = param.shape[0]
    outs = 2 * rows
    half = width // 2
    scale = 1.0 / math.sqrt(3.0 * width)
    total_rows = seqs * span * 256
    eta = math.sqrt(3.0 * width / total_rows)
    core, ylo, yhi, x, z = (lax.axis_index(a) for a in ("core", "ylo", "yhi", "x", "z"))
    y = 2 * yhi + ylo
    first = core == 0
    me = jnp.where(first, x, y)
    over = jnp.where(first, y, x)

    edge = jnp.where(first, inputs[:, :D], inputs[:, span - D :])
    edge = lax.ppermute(edge, SEQ, outward())

    mate = swap(cotangent)
    chip = jnp.concatenate(
        [jnp.where(first, cotangent, mate), jnp.where(first, mate, cotangent)], axis=1
    )
    cots = [lax.dynamic_slice_in_dim(chip, lax.rem(me + d, 4) * outs, outs, 2) for d in range(4)]
    cots = [cots[0]] + [lax.ppermute(cots[d], PLANE, along(d)) for d in range(1, 4)]

    own = normalise(inputs, gain)
    edge = normalise(edge, gain)
    ext = jnp.where(
        first, jnp.concatenate([edge, own], axis=1), jnp.concatenate([own, edge], axis=1)
    )
    low, high = ext[:, :, :half], ext[:, :, half:]
    mine = jnp.where(first, low, high)
    mate = swap(jnp.where(first, high, low))
    block = jnp.concatenate([jnp.where(first, mine, mate), jnp.where(first, mate, mine)], axis=1)

    blocks = [block] + [lax.ppermute(block, PLANE, along(d)) for d in (1, 2, 3)]

    at_over = over.astype(jnp.int32).reshape(1)
    sums = 2 * 4 * seqs * 2 * span * outs * half * 3
    turned = call(
        turn_kernel, [jax.ShapeDtypeStruct((outs, seqs * 2 * span), BF16)] * 4, (), cots, 0
    )
    quarter = half // 2
    (grad,) = call(
        functools.partial(grad_kernel, scale),
        [jax.ShapeDtypeStruct((4, 3 * rows, quarter), BF16)],
        (at_over,),
        (*turned, *blocks),
        sums,
    )
    kernel = jnp.transpose(param, (1, 0, 2))
    share = lax.dynamic_slice_in_dim(kernel, core * half, half, 2)
    grad, share = lax.optimization_barrier((grad, share))
    terms = [grad[0]] + [lax.ppermute(grad[d], PLANE, across(d)) for d in range(1, 4)]
    summed = sum(t.astype(F32) for t in terms).astype(BF16)
    piece = 3 * rows // 8
    terms = lax.all_to_all(summed.reshape(8, piece, quarter), "z", 0, 0, tiled=True)
    summed = jnp.sum(terms.astype(F32), axis=0).astype(BF16)
    summed = lax.ppermute(
        summed, PLANE, plane_perm(lambda c, x, y: (x, y) if c == 0 else (y, x))
    )
    at = (z * piece, core * half + ylo * quarter)
    own_param = lax.dynamic_slice(kernel.reshape(3 * rows, width), at, (piece, quarter))
    own_noise = lax.dynamic_slice(
        jnp.transpose(noise, (1, 0, 2)).reshape(3 * rows, width), at, (piece, quarter)
    )
    new = (
        own_param.astype(F32)
        - eta * summed.astype(F32)
        + math.sqrt(2.0 * eta) * own_noise.astype(F32)
    ).astype(BF16)
    new = jnp.broadcast_to(new[None], (16, piece, quarter))
    new = lax.all_to_all(new, ("z", "ylo"), 0, 0, tiled=True)
    new = jnp.transpose(new.reshape(8, 2, piece, quarter), (0, 2, 1, 3)).reshape(3 * rows, half)
    mate = swap(new)
    new = jnp.concatenate([jnp.where(first, new, mate), jnp.where(first, mate, new)], axis=1)
    new_param = jnp.transpose(new.reshape(3, rows, width), (1, 0, 2))

    one = lax.ppermute(share, PLANE, plane_perm(lambda c, x, y: (x, y) if c == 0 else (y, x)))
    two = lax.ppermute(
        share, PLANE, plane_perm(lambda c, x, y: (x, 3 - y) if c == 0 else (y + 2, x))
    )
    mixed = call(
        functools.partial(mixed_kernel, scale),
        [jax.ShapeDtypeStruct((seqs, 2 * span, outs), BF16)] * 4,
        (at_over,),
        (one, two, *blocks),
        sums,
        [pltpu.VMEM((3, outs, half), BF16)],
    )
    back = [mixed[0]] + [lax.ppermute(mixed[d], PLANE, along(-d)) for d in range(1, 4)]
    total = jnp.zeros((seqs, 2 * span, width), BF16)
    for d in range(4):
        total = lax.dynamic_update_slice_in_dim(total, back[d], lax.rem(me + d, 4) * outs, 2)
    near, away = total[:, :span], total[:, span:]
    mate = swap(jnp.where(first, away, near))
    near = jnp.where(first, near, away)
    outputs = (inputs.astype(F32) + (near.astype(F32) + mate.astype(F32))).astype(BF16)
    return (outputs, new_param)


def solution(mesh):
    fine = Mesh(mesh.devices.reshape(8, 2, 2, 4, 2), ("z", "ylo", "core", "x", "yhi"))
    spread = P(("x", "yhi"), SEQ, None)
    placed = (spread, P(), P(("x", "yhi"), None, None), spread, P(("x", "yhi"), None, None))
    return jax.shard_map(
        shards,
        mesh=fine,
        in_specs=placed,
        out_specs=(spread, P(("x", "yhi"), None, None)),
        check_vma=False,
    )
```

```python
import functools
import math

import jax
import jax.numpy as jnp
from jax import lax
from jax.experimental import pallas as pl
from jax.experimental.pallas import tpu as pltpu
from jax.sharding import Mesh, PartitionSpec as P

D = 16
F32, BF16 = jnp.float32, jnp.bfloat16
SEQ = ("z", "ylo", "core")
PLANE = ("ylo", "yhi")


def around_x(step):
    return [(i, (i + step) % 4) for i in range(4)]


def around_y(step):
    at = [(y % 2) * 2 + y // 2 for y in range(4)]
    return [(at[y], at[(y + step) % 4]) for y in range(4)]


def other_y():
    at = [(y % 2) * 2 + y // 2 for y in range(4)]
    return [(at[y], at[3 - y]) for y in range(4)]


def outward():
    n = lax.axis_size(SEQ)
    pairs = []
    for i in range(n):
        j = i - 1 if i % 2 == 0 else i + 1
        if 0 <= j < n:
            pairs.append((i, j))
    return pairs


def swap(v):
    return lax.ppermute(v, "core", [(0, 1), (1, 0)])


def normalise(values, gain):
    floats = values.astype(F32)
    factor = lax.rsqrt(jnp.mean(floats * floats, axis=-1, keepdims=True) + 1e-06)
    return jax.nn.gelu(floats * factor * gain).astype(BF16)


def in_vmem(count):
    return [pl.BlockSpec(memory_space=pltpu.VMEM)] * count


def call(kernel, shapes, scalars, arrays, flops, scratch=()):
    size = sum(math.prod(a.shape) * a.dtype.itemsize for a in (*arrays, *shapes))
    return pl.pallas_call(
        kernel,
        out_shape=shapes,
        in_specs=[pl.BlockSpec(memory_space=pltpu.SMEM)] * len(scalars) + in_vmem(len(arrays)),
        out_specs=in_vmem(len(shapes)),
        scratch_shapes=list(scratch),
        cost_estimate=pl.CostEstimate(flops=flops, bytes_accessed=size, transcendentals=0),
        compiler_params=pltpu.CompilerParams(vmem_limit_bytes=40 * 2**20),
    )(*scalars, *arrays)


ORDER = (0, 1, 3, 2)


def turn_kernel(x, source, *targets):
    n = source.shape[1] - 2 * D
    for k, target in enumerate(targets):
        for i, d in enumerate(ORDER):
            for b in range(2):
                place = ((x[0] - d) & 3) * 2 + b
                at = (2 * i + b) * n
                target[:, at : at + n] = source[place, (2 - k) * D : (2 - k) * D + n].T


def sequences(blocks):
    return [ref.at[b] for ref in blocks for b in range(ref.shape[0])]


def near_grad_kernel(*refs):
    turned, blocks, out = refs[:3], sequences(refs[3:-1]), refs[-1]
    n, width = blocks[0].shape
    tile = 256
    for k in range(3):
        for at in range(0, width, tile):
            total = jnp.zeros((out.shape[1], tile), F32)
            for b, block in enumerate(blocks):
                total += jnp.dot(
                    turned[k][:, b * n : (b + 1) * n],
                    block[:, at : at + tile],
                    preferred_element_type=F32,
                )
            out[k, :, at : at + tile] = total


def grad_kernel(scale, over, sums, *refs):
    turned, blocks, out = refs[:3], sequences(refs[3:-1]), refs[-1]
    outs = turned[0].shape[0]
    rows = outs // 2
    n, width = blocks[0].shape
    quarter, tile = width // 2, 256
    seen = turned[0].shape[1] - len(blocks) * n
    for k in range(3):
        for at in range(0, width, tile):
            total = sums[k, :, at : at + tile]
            for b, block in enumerate(blocks):
                total += jnp.dot(
                    turned[k][:, seen + b * n : seen + (b + 1) * n],
                    block[:, at : at + tile],
                    preferred_element_type=F32,
                )
            total = (total * scale).astype(BF16)
            for sub in range(2):
                lo, hi = max(at, sub * quarter), min(at + tile, (sub + 1) * quarter)
                if lo >= hi:
                    continue
                for part in range(2):
                    slot = (2 * part + sub - over[0] + 4) & 3
                    out[slot, k * rows : (k + 1) * rows, lo - sub * quarter : hi - sub * quarter] = (
                        total[part * rows : (part + 1) * rows, lo - at : hi - at]
                    )


def mixed_kernel(scale, over, one, two, *refs):
    blocks, (result, weights, total) = sequences(refs[:-3]), refs[-3:]
    rows, n = one.shape[1], blocks[0].shape[0]
    swapped = jnp.where(over[0] < 2, 0, rows)
    for k in range(3):
        weights[k, pl.ds(pl.multiple_of(swapped, rows), rows), :] = one[k]
        weights[k, pl.ds(pl.multiple_of(rows - swapped, rows), rows), :] = two[k]
    for b, block in enumerate(blocks):
        for k in (0, 2, 1):
            part = lax.dot_general(
                block[...], weights[k], (((1,), (1,)), ((), ())), preferred_element_type=F32
            )
            if k == 0:
                total[2 * D :] = part
            elif k == 2:
                total[: 2 * D] = part[: 2 * D]
                total[2 * D : n] += part[2 * D :]
            else:
                total[D : D + n] += part
        result[b] = (total[...] * scale).astype(BF16)


def shards(inputs, gain, param, cotangent, noise):
    seqs, span, width = inputs.shape
    rows = param.shape[0]
    outs = 2 * rows
    half = width // 2
    quarter = half // 2
    piece = 3 * rows // 8
    scale = 1.0 / math.sqrt(3.0 * width)
    total_rows = seqs * span * 256
    eta = math.sqrt(3.0 * width / total_rows)
    core, ylo, yhi, x, z = (lax.axis_index(a) for a in ("core", "ylo", "yhi", "x", "z"))
    y = 2 * yhi + ylo
    first = core == 0
    at_x = x.astype(jnp.int32).reshape(1)
    at_y = y.astype(jnp.int32).reshape(1)

    edge = jnp.where(first, cotangent[:, :D], cotangent[:, span - D :])
    values, edge = lax.optimization_barrier((inputs, edge))
    edge = lax.ppermute(edge, SEQ, outward())
    cot = jnp.where(
        first,
        jnp.concatenate([edge, cotangent], axis=1),
        jnp.concatenate([cotangent, edge], axis=1),
    )
    cot = jnp.transpose(cot.reshape(seqs, span + D, 4, outs), (2, 0, 1, 3))
    cot = lax.all_to_all(cot.reshape(8, span + D, outs), "x", 0, 0, tiled=True)

    own = normalise(values, gain)
    low, high = own[:, :, :half], own[:, :, half:]
    mine = jnp.where(first, low, high)
    mate = swap(jnp.where(first, high, low))
    block = jnp.concatenate([jnp.where(first, mine, mate), jnp.where(first, mate, mine)], axis=1)
    left = lax.ppermute(block, "x", around_x(1))
    right = lax.ppermute(block, "x", around_x(-1))
    far = [lax.ppermute(left[:1], "x", around_x(1)), lax.ppermute(right[1:], "x", around_x(-1))]
    kernel = jnp.transpose(param, (1, 0, 2))
    block, kernel = lax.optimization_barrier((block, kernel))
    share = lax.dynamic_slice_in_dim(kernel, core * half, half, 2)
    other = lax.ppermute(share, PLANE, other_y())

    cot, other, left, right = lax.optimization_barrier((cot, other, left, right))
    mate = swap(cot)
    cot = jnp.concatenate([jnp.where(first, cot, mate), jnp.where(first, mate, cot)], axis=1)
    turned = call(
        turn_kernel, [jax.ShapeDtypeStruct((outs, 8 * 2 * span), BF16)] * 3, (at_x,), (cot,), 0
    )

    work = 2 * 2 * span * outs * half * 3
    (sums,) = call(
        near_grad_kernel,
        [jax.ShapeDtypeStruct((3, outs, half), F32)],
        (),
        (*turned, block, left, right),
        6 * work,
    )
    far, sums = lax.optimization_barrier((far, sums))
    (grad,) = call(
        functools.partial(grad_kernel, scale),
        [jax.ShapeDtypeStruct((4, 3 * rows, quarter), BF16)],
        (at_y,),
        (sums, *turned, *far),
        2 * work,
    )
    grad, far = lax.optimization_barrier((grad, far))
    terms = [grad[0]] + [lax.ppermute(grad[d], PLANE, around_y(d)) for d in range(1, 4)]
    summed = sum(t.astype(F32) for t in terms).astype(BF16)

    terms = lax.all_to_all(summed.reshape(8, piece, quarter), "z", 0, 0, tiled=True)

    mixed = []
    for group in ((block, left, right), far):
        (part,) = call(
            functools.partial(mixed_kernel, scale),
            [jax.ShapeDtypeStruct((sum(g.shape[0] for g in group), 2 * (span + D), outs), BF16)],
            (at_y,),
            (share, other, *group),
            0,
            [pltpu.VMEM((3, outs, half), BF16), pltpu.VMEM((2 * (span + D), outs), F32)],
        )
        mixed.append(part)
    near = jnp.concatenate([m[:, : span + D] for m in mixed], axis=0)
    away = jnp.concatenate([m[:, span + D :] for m in mixed], axis=0)
    mate = swap(jnp.where(first, away, near))
    total = jnp.where(first, near, away).astype(F32) + mate.astype(F32)
    edge = jnp.where(first, total[:, :D], total[:, span:]).astype(BF16)
    edge = lax.ppermute(edge, SEQ, outward())
    terms, edge = lax.optimization_barrier((terms, edge))
    edge = edge.astype(F32)
    total = jnp.where(
        first,
        jnp.concatenate([total[:, D : 2 * D] + edge, total[:, 2 * D :]], axis=1),
        jnp.concatenate([total[:, : span - D], total[:, span - D : span] + edge], axis=1),
    )
    total = total.astype(BF16).reshape(4, seqs, span, outs)
    back = [total[0]] + [
        lax.ppermute(total[i], "x", around_x(-d)) for i, d in enumerate(ORDER) if d > 0
    ]

    summed = jnp.sum(terms.astype(F32), axis=0)
    at = (z * piece, core * half + ylo * quarter)
    own_param = lax.dynamic_slice(kernel.reshape(3 * rows, width), at, (piece, quarter))
    own_noise = lax.dynamic_slice(
        jnp.transpose(noise, (1, 0, 2)).reshape(3 * rows, width), at, (piece, quarter)
    )
    new = (
        own_param.astype(F32) - eta * summed + math.sqrt(2.0 * eta) * own_noise.astype(F32)
    ).astype(BF16)
    copies = jnp.broadcast_to(new[None], (16, piece, quarter))
    sent = lax.all_to_all(copies, ("z", "ylo"), 0, 0, tiled=True)

    back, sent = lax.optimization_barrier((back, sent))
    result = jnp.zeros((seqs, span, width), BF16)
    for rows_back, d in zip(back, ORDER):
        result = lax.dynamic_update_slice_in_dim(result, rows_back, lax.rem(x + d, 4) * outs, 2)
    outputs = (inputs.astype(F32) + result.astype(F32)).astype(BF16)

    sent = jnp.transpose(sent.reshape(8, 2, piece, quarter), (0, 2, 1, 3)).reshape(3 * rows, half)
    mate = swap(sent)
    sent = jnp.concatenate([jnp.where(first, sent, mate), jnp.where(first, mate, sent)], axis=1)
    new_param = jnp.transpose(sent.reshape(3, rows, width), (1, 0, 2))
    return (outputs, new_param)


def solution(mesh):
    fine = Mesh(mesh.devices.reshape(8, 2, 2, 4, 2), ("z", "ylo", "core", "x", "yhi"))
    spread = P(("x", "yhi"), SEQ, None)
    placed = (spread, P(), P(("x", "yhi"), None, None), spread, P(("x", "yhi"), None, None))
    return jax.shard_map(
        shards,
        mesh=fine,
        in_specs=placed,
        out_specs=(spread, P(("x", "yhi"), None, None)),
        check_vma=False,
    )
```

```python
import functools
import math

import jax
import jax.numpy as jnp
from jax import lax
from jax.experimental import pallas as pl
from jax.experimental.pallas import tpu as pltpu
from jax.sharding import Mesh, PartitionSpec as P

D = 16
F32, BF16 = jnp.float32, jnp.bfloat16
SEQ = ("z", "ylo", "core")
PLANE = ("ylo", "yhi")


def around_x(step):
    return [(i, (i + step) % 4) for i in range(4)]


def around_y(step):
    at = [(y % 2) * 2 + y // 2 for y in range(4)]
    return [(at[y], at[(y + step) % 4]) for y in range(4)]


def other_y():
    at = [(y % 2) * 2 + y // 2 for y in range(4)]
    return [(at[y], at[3 - y]) for y in range(4)]


def outward():
    n = lax.axis_size(SEQ)
    pairs = []
    for i in range(n):
        j = i - 1 if i % 2 == 0 else i + 1
        if 0 <= j < n:
            pairs.append((i, j))
    return pairs


def swap(v):
    return lax.ppermute(v, "core", [(0, 1), (1, 0)])


def normalise(values, gain):
    floats = values.astype(F32)
    factor = lax.rsqrt(jnp.mean(floats * floats, axis=-1, keepdims=True) + 1e-06)
    return jax.nn.gelu(floats * factor * gain).astype(BF16)


def in_vmem(count):
    return [pl.BlockSpec(memory_space=pltpu.VMEM)] * count


def call(kernel, shapes, scalars, arrays, flops, scratch=()):
    size = sum(math.prod(a.shape) * a.dtype.itemsize for a in (*arrays, *shapes))
    return pl.pallas_call(
        kernel,
        out_shape=shapes,
        in_specs=[pl.BlockSpec(memory_space=pltpu.SMEM)] * len(scalars) + in_vmem(len(arrays)),
        out_specs=in_vmem(len(shapes)),
        scratch_shapes=list(scratch),
        cost_estimate=pl.CostEstimate(flops=flops, bytes_accessed=size, transcendentals=0),
        compiler_params=pltpu.CompilerParams(vmem_limit_bytes=40 * 2**20),
    )(*scalars, *arrays)


ORDER = (0, 1, 3, 2)


def turn_kernel(x, source, *targets):
    n = source.shape[1] - 2 * D
    for k, target in enumerate(targets):
        for i, d in enumerate(ORDER):
            for b in range(2):
                place = ((x[0] - d) & 3) * 2 + b
                at = (2 * i + b) * n
                target[:, at : at + n] = source[place, (2 - k) * D : (2 - k) * D + n].T


def sequences(blocks):
    return [ref.at[b] for ref in blocks for b in range(ref.shape[0])]


def near_grad_kernel(*refs):
    turned, blocks, out = refs[:3], sequences(refs[3:-1]), refs[-1]
    n, width = blocks[0].shape
    tile = 256
    for k in range(3):
        for at in range(0, width, tile):
            total = jnp.zeros((out.shape[1], tile), F32)
            for b, block in enumerate(blocks):
                total += jnp.dot(
                    turned[k][:, b * n : (b + 1) * n],
                    block[:, at : at + tile],
                    preferred_element_type=F32,
                )
            out[k, :, at : at + tile] = total


def grad_kernel(scale, over, sums, *refs):
    turned, blocks, out = refs[:3], sequences(refs[3:-1]), refs[-1]
    outs = turned[0].shape[0]
    rows = outs // 2
    n, width = blocks[0].shape
    quarter, tile = width // 2, 256
    seen = turned[0].shape[1] - len(blocks) * n
    for k in range(3):
        for at in range(0, width, tile):
            total = sums[k, :, at : at + tile]
            for b, block in enumerate(blocks):
                total += jnp.dot(
                    turned[k][:, seen + b * n : seen + (b + 1) * n],
                    block[:, at : at + tile],
                    preferred_element_type=F32,
                )
            total = (total * scale).astype(BF16)
            for sub in range(2):
                lo, hi = max(at, sub * quarter), min(at + tile, (sub + 1) * quarter)
                if lo >= hi:
                    continue
                for part in range(2):
                    slot = (2 * part + sub - over[0] + 4) & 3
                    out[slot, k * rows : (k + 1) * rows, lo - sub * quarter : hi - sub * quarter] = (
                        total[part * rows : (part + 1) * rows, lo - at : hi - at]
                    )


def update_kernel(eta, terms, param, noise, out):
    total = jnp.sum(terms[...].astype(F32), axis=0)
    new = (
        param[...].astype(F32) - eta * total + math.sqrt(2.0 * eta) * noise[...].astype(F32)
    ).astype(BF16)
    for i in range(out.shape[0]):
        out[i] = new


def place_kernel(core, own, mate, out):
    rows, columns = own.shape[1:]
    for source, side in ((own, core[0]), (mate, 1 - core[0])):
        for i in range(own.shape[0]):
            start = pl.multiple_of(side * (2 * columns) + (i % 2) * columns, columns)
            out[(i // 2) * rows : (i // 2 + 1) * rows, pl.ds(start, columns)] = source[i]


def mixed_kernel(scale, over, one, two, *refs):
    blocks, (result, weights, total) = sequences(refs[:-3]), refs[-3:]
    rows, n = one.shape[1], blocks[0].shape[0]
    swapped = jnp.where(over[0] < 2, 0, rows)
    for k in range(3):
        weights[k, pl.ds(pl.multiple_of(swapped, rows), rows), :] = one[k]
        weights[k, pl.ds(pl.multiple_of(rows - swapped, rows), rows), :] = two[k]
    for b, block in enumerate(blocks):
        for k in (0, 2, 1):
            part = lax.dot_general(
                block[...], weights[k], (((1,), (1,)), ((), ())), preferred_element_type=F32
            )
            if k == 0:
                total[2 * D :] = part
            elif k == 2:
                total[: 2 * D] = part[: 2 * D]
                total[2 * D : n] += part[2 * D :]
            else:
                total[D : D + n] += part
        result[b] = (total[...] * scale).astype(BF16)


def shards(inputs, gain, param, cotangent, noise):
    seqs, span, width = inputs.shape
    rows = param.shape[0]
    outs = 2 * rows
    half = width // 2
    quarter = half // 2
    piece = 3 * rows // 8
    scale = 1.0 / math.sqrt(3.0 * width)
    total_rows = seqs * span * 256
    eta = math.sqrt(3.0 * width / total_rows)
    core, ylo, yhi, x, z = (lax.axis_index(a) for a in ("core", "ylo", "yhi", "x", "z"))
    y = 2 * yhi + ylo
    first = core == 0
    at_x = x.astype(jnp.int32).reshape(1)
    at_y = y.astype(jnp.int32).reshape(1)

    edge = jnp.where(first, cotangent[:, :D], cotangent[:, span - D :])
    values, edge = lax.optimization_barrier((inputs, edge))
    edge = lax.ppermute(edge, SEQ, outward())
    cot = jnp.where(
        first,
        jnp.concatenate([edge, cotangent], axis=1),
        jnp.concatenate([cotangent, edge], axis=1),
    )
    cot = jnp.transpose(cot.reshape(seqs, span + D, 4, outs), (2, 0, 1, 3))
    cot = lax.all_to_all(cot.reshape(8, span + D, outs), "x", 0, 0, tiled=True)

    own = normalise(values, gain)
    low, high = own[:, :, :half], own[:, :, half:]
    mine = jnp.where(first, low, high)
    mate = swap(jnp.where(first, high, low))
    block = jnp.concatenate([jnp.where(first, mine, mate), jnp.where(first, mate, mine)], axis=1)
    left = lax.ppermute(block, "x", around_x(1))
    right = lax.ppermute(block, "x", around_x(-1))
    far = [lax.ppermute(left[:1], "x", around_x(1)), lax.ppermute(right[1:], "x", around_x(-1))]
    kernel = jnp.transpose(param, (1, 0, 2))
    block, kernel = lax.optimization_barrier((block, kernel))
    share = lax.dynamic_slice_in_dim(kernel, core * half, half, 2)
    other = lax.ppermute(share, PLANE, other_y())

    cot, other, left, right = lax.optimization_barrier((cot, other, left, right))
    mate = swap(cot)
    cot = jnp.concatenate([jnp.where(first, cot, mate), jnp.where(first, mate, cot)], axis=1)
    turned = call(
        turn_kernel, [jax.ShapeDtypeStruct((outs, 8 * 2 * span), BF16)] * 3, (at_x,), (cot,), 0
    )

    work = 2 * 2 * span * outs * half * 3
    (sums,) = call(
        near_grad_kernel,
        [jax.ShapeDtypeStruct((3, outs, half), F32)],
        (),
        (*turned, block, left, right),
        6 * work,
    )
    far, sums = lax.optimization_barrier((far, sums))
    (grad,) = call(
        functools.partial(grad_kernel, scale),
        [jax.ShapeDtypeStruct((4, 3 * rows, quarter), BF16)],
        (at_y,),
        (sums, *turned, *far),
        2 * work,
    )
    grad, far = lax.optimization_barrier((grad, far))
    terms = [grad[0]] + [lax.ppermute(grad[d], PLANE, around_y(d)) for d in range(1, 4)]
    summed = sum(t.astype(F32) for t in terms).astype(BF16)

    terms = lax.all_to_all(summed.reshape(8, piece, quarter), "z", 0, 0, tiled=True)

    mixed = []
    for group in ((block, left, right), far):
        (part,) = call(
            functools.partial(mixed_kernel, scale),
            [jax.ShapeDtypeStruct((sum(g.shape[0] for g in group), 2 * (span + D), outs), BF16)],
            (at_y,),
            (share, other, *group),
            0,
            [pltpu.VMEM((3, outs, half), BF16), pltpu.VMEM((2 * (span + D), outs), F32)],
        )
        mixed.append(part)
    near = jnp.concatenate([m[:, : span + D] for m in mixed], axis=0)
    away = jnp.concatenate([m[:, span + D :] for m in mixed], axis=0)
    mate = swap(jnp.where(first, away, near))
    total = jnp.where(first, near, away).astype(F32) + mate.astype(F32)
    edge = jnp.where(first, total[:, :D], total[:, span:]).astype(BF16)
    edge = lax.ppermute(edge, SEQ, outward())
    terms, edge = lax.optimization_barrier((terms, edge))
    edge = edge.astype(F32)
    total = jnp.where(
        first,
        jnp.concatenate([total[:, D : 2 * D] + edge, total[:, 2 * D :]], axis=1),
        jnp.concatenate([total[:, : span - D], total[:, span - D : span] + edge], axis=1),
    )
    total = total.astype(BF16).reshape(4, seqs, span, outs)
    back = [total[0]] + [
        lax.ppermute(total[i], "x", around_x(-d)) for i, d in enumerate(ORDER) if d > 0
    ]

    at = (z * piece, core * half + ylo * quarter)
    own_param = lax.dynamic_slice(kernel.reshape(3 * rows, width), at, (piece, quarter))
    own_noise = lax.dynamic_slice(
        jnp.transpose(noise, (1, 0, 2)).reshape(3 * rows, width), at, (piece, quarter)
    )
    (copies,) = call(
        functools.partial(update_kernel, eta),
        [jax.ShapeDtypeStruct((16, piece, quarter), BF16)],
        (),
        (terms, own_param, own_noise),
        0,
    )
    sent = lax.all_to_all(copies, ("z", "ylo"), 0, 0, tiled=True)

    back, sent = lax.optimization_barrier((back, sent))
    result = jnp.zeros((seqs, span, width), BF16)
    for rows_back, d in zip(back, ORDER):
        result = lax.dynamic_update_slice_in_dim(result, rows_back, lax.rem(x + d, 4) * outs, 2)
    outputs = (inputs.astype(F32) + result.astype(F32)).astype(BF16)

    (sent,) = call(
        place_kernel,
        [jax.ShapeDtypeStruct((3 * rows, width), BF16)],
        (core.astype(jnp.int32).reshape(1),),
        (sent, swap(sent)),
        0,
    )
    new_param = jnp.transpose(sent.reshape(3, rows, width), (1, 0, 2))
    return (outputs, new_param)


def solution(mesh):
    fine = Mesh(mesh.devices.reshape(8, 2, 2, 4, 2), ("z", "ylo", "core", "x", "yhi"))
    spread = P(("x", "yhi"), SEQ, None)
    placed = (spread, P(), P(("x", "yhi"), None, None), spread, P(("x", "yhi"), None, None))
    return jax.shard_map(
        shards,
        mesh=fine,
        in_specs=placed,
        out_specs=(spread, P(("x", "yhi"), None, None)),
        check_vma=False,
    )
```

```python
import functools
import math

import jax
import jax.numpy as jnp
from jax import lax
from jax.experimental import pallas as pl
from jax.experimental.pallas import tpu as pltpu
from jax.sharding import Mesh, PartitionSpec as P

D = 16
F32, BF16 = jnp.float32, jnp.bfloat16
SEQ = ("z", "ylo", "core")
PLANE = ("ylo", "yhi")


def around_x(step):
    return [(i, (i + step) % 4) for i in range(4)]


def around_y(step):
    at = [(y % 2) * 2 + y // 2 for y in range(4)]
    return [(at[y], at[(y + step) % 4]) for y in range(4)]


def other_y():
    at = [(y % 2) * 2 + y // 2 for y in range(4)]
    return [(at[y], at[3 - y]) for y in range(4)]


def outward():
    n = lax.axis_size(SEQ)
    pairs = []
    for i in range(n):
        j = i - 1 if i % 2 == 0 else i + 1
        if 0 <= j < n:
            pairs.append((i, j))
    return pairs


def swap(v):
    return lax.ppermute(v, "core", [(0, 1), (1, 0)])


def normalise(values, gain):
    floats = values.astype(F32)
    factor = lax.rsqrt(jnp.mean(floats * floats, axis=-1, keepdims=True) + 1e-06)
    return jax.nn.gelu(floats * factor * gain).astype(BF16)


def in_vmem(count):
    return [pl.BlockSpec(memory_space=pltpu.VMEM)] * count


def call(kernel, shapes, scalars, arrays, flops, scratch=()):
    size = sum(math.prod(a.shape) * a.dtype.itemsize for a in (*arrays, *shapes))
    return pl.pallas_call(
        kernel,
        out_shape=shapes,
        in_specs=[pl.BlockSpec(memory_space=pltpu.SMEM)] * len(scalars) + in_vmem(len(arrays)),
        out_specs=in_vmem(len(shapes)),
        scratch_shapes=list(scratch),
        cost_estimate=pl.CostEstimate(flops=flops, bytes_accessed=size, transcendentals=0),
        compiler_params=pltpu.CompilerParams(vmem_limit_bytes=40 * 2**20),
    )(*scalars, *arrays)


ORDER = (0, 1, 3, 2)


def turn_kernel(x, core, own, mate, *targets):
    n = 2 * own.shape[1] - 2 * D
    low = core[0] == 0
    for i, d in enumerate(ORDER):
        for b in range(2):
            place = ((x[0] - d) & 3) * 2 + b
            mine, other = own[place], mate[place]
            rows = jnp.concatenate(
                [jnp.where(low, mine, other), jnp.where(low, other, mine)], axis=0
            )
            at = (2 * i + b) * n
            for k, target in enumerate(targets):
                target[:, at : at + n] = rows[(2 - k) * D : (2 - k) * D + n].T


def sequences(blocks):
    return [ref.at[b] for ref in blocks for b in range(ref.shape[0])]


def near_grad_kernel(*refs):
    turned, blocks, out = refs[:3], sequences(refs[3:-1]), refs[-1]
    n, width = blocks[0].shape
    tile = 256
    for k in range(3):
        for at in range(0, width, tile):
            total = jnp.zeros((out.shape[1], tile), F32)
            for b, block in enumerate(blocks):
                total += jnp.dot(
                    turned[k][:, b * n : (b + 1) * n],
                    block[:, at : at + tile],
                    preferred_element_type=F32,
                )
            out[k, :, at : at + tile] = total


def grad_kernel(scale, over, sums, *refs):
    turned, blocks, out = refs[:3], sequences(refs[3:-1]), refs[-1]
    outs = turned[0].shape[0]
    rows = outs // 2
    n, width = blocks[0].shape
    quarter, tile = width // 2, 256
    seen = turned[0].shape[1] - len(blocks) * n
    for k in range(3):
        for at in range(0, width, tile):
            total = sums[k, :, at : at + tile]
            for b, block in enumerate(blocks):
                total += jnp.dot(
                    turned[k][:, seen + b * n : seen + (b + 1) * n],
                    block[:, at : at + tile],
                    preferred_element_type=F32,
                )
            total = (total * scale).astype(BF16)
            for sub in range(2):
                lo, hi = max(at, sub * quarter), min(at + tile, (sub + 1) * quarter)
                if lo >= hi:
                    continue
                for part in range(2):
                    slot = (2 * part + sub - over[0] + 4) & 3
                    out[slot, k * rows : (k + 1) * rows, lo - sub * quarter : hi - sub * quarter] = (
                        total[part * rows : (part + 1) * rows, lo - at : hi - at]
                    )


def update_kernel(eta, terms, param, noise, out):
    total = jnp.sum(terms[...].astype(F32), axis=0)
    new = (
        param[...].astype(F32) - eta * total + math.sqrt(2.0 * eta) * noise[...].astype(F32)
    ).astype(BF16)
    for i in range(out.shape[0]):
        out[i] = new


def place_kernel(core, own, mate, out):
    rows, columns = own.shape[1:]
    for source, side in ((own, core[0]), (mate, 1 - core[0])):
        for i in range(own.shape[0]):
            start = pl.multiple_of(side * (2 * columns) + (i % 2) * columns, columns)
            out[(i // 2) * rows : (i // 2 + 1) * rows, pl.ds(start, columns)] = source[i]


def near_mixed_kernel(scale, over, one, two, *refs):
    weights = refs[-2]
    rows = one.shape[1]
    swapped = jnp.where(over[0] < 2, 0, rows)
    for k in range(3):
        weights[k, pl.ds(pl.multiple_of(swapped, rows), rows), :] = one[k]
        weights[k, pl.ds(pl.multiple_of(rows - swapped, rows), rows), :] = two[k]
    mixed_kernel(scale, weights, *refs[:-2], refs[-1])


def mixed_kernel(scale, weights, *refs):
    blocks, (result, total) = sequences(refs[:-2]), refs[-2:]
    n = blocks[0].shape[0]
    for b, block in enumerate(blocks):
        for k in (0, 2, 1):
            part = lax.dot_general(
                block[...], weights[k], (((1,), (1,)), ((), ())), preferred_element_type=F32
            )
            if k == 0:
                total[2 * D :] = part
            elif k == 2:
                total[: 2 * D] = part[: 2 * D]
                total[2 * D : n] += part[2 * D :]
            else:
                total[D : D + n] += part
        result[b] = (total[...] * scale).astype(BF16)


def shards(inputs, gain, param, cotangent, noise):
    seqs, span, width = inputs.shape
    rows = param.shape[0]
    outs = 2 * rows
    half = width // 2
    quarter = half // 2
    piece = 3 * rows // 8
    scale = 1.0 / math.sqrt(3.0 * width)
    total_rows = seqs * span * 256
    eta = math.sqrt(3.0 * width / total_rows)
    core, ylo, yhi, x, z = (lax.axis_index(a) for a in ("core", "ylo", "yhi", "x", "z"))
    y = 2 * yhi + ylo
    first = core == 0
    at_x = x.astype(jnp.int32).reshape(1)
    at_y = y.astype(jnp.int32).reshape(1)

    edge = jnp.where(first, cotangent[:, :D], cotangent[:, span - D :])
    values, edge = lax.optimization_barrier((inputs, edge))
    edge = lax.ppermute(edge, SEQ, outward())
    cot = jnp.where(
        first,
        jnp.concatenate([edge, cotangent], axis=1),
        jnp.concatenate([cotangent, edge], axis=1),
    )
    cot = jnp.transpose(cot.reshape(seqs, span + D, 4, outs), (2, 0, 1, 3))
    cot = lax.all_to_all(cot.reshape(8, span + D, outs), "x", 0, 0, tiled=True)

    own = normalise(values, gain)
    low, high = own[:, :, :half], own[:, :, half:]
    mine = jnp.where(first, low, high)
    mate = swap(jnp.where(first, high, low))
    block = jnp.concatenate([jnp.where(first, mine, mate), jnp.where(first, mate, mine)], axis=1)
    left = lax.ppermute(block, "x", around_x(1))
    right = lax.ppermute(block, "x", around_x(-1))
    far = [lax.ppermute(left[:1], "x", around_x(1)), lax.ppermute(right[1:], "x", around_x(-1))]
    kernel = jnp.transpose(param, (1, 0, 2))
    block, kernel = lax.optimization_barrier((block, kernel))
    share = lax.dynamic_slice_in_dim(kernel, core * half, half, 2)
    other = lax.ppermute(share, PLANE, other_y())

    cot, other, left, right = lax.optimization_barrier((cot, other, left, right))
    at_core = core.astype(jnp.int32).reshape(1)
    turned = call(
        turn_kernel, [jax.ShapeDtypeStruct((outs, 8 * 2 * span), BF16)] * 3, (at_x, at_core), (cot, swap(cot)), 0
    )

    work = 2 * 2 * span * outs * half * 3
    (sums,) = call(
        near_grad_kernel,
        [jax.ShapeDtypeStruct((3, outs, half), F32)],
        (),
        (*turned, block, left, right),
        6 * work,
    )
    far, sums = lax.optimization_barrier((far, sums))
    (grad,) = call(
        functools.partial(grad_kernel, scale),
        [jax.ShapeDtypeStruct((4, 3 * rows, quarter), BF16)],
        (at_y,),
        (sums, *turned, *far),
        2 * work,
    )
    grad, far = lax.optimization_barrier((grad, far))
    terms = [grad[0]] + [lax.ppermute(grad[d], PLANE, around_y(d)) for d in range(1, 4)]
    summed = sum(t.astype(F32) for t in terms).astype(BF16)

    terms = lax.all_to_all(summed.reshape(8, piece, quarter), "z", 0, 0, tiled=True)

    sums_at = pltpu.VMEM((2 * (span + D), outs), F32)
    near_mixed, weights = call(
        functools.partial(near_mixed_kernel, scale),
        [
            jax.ShapeDtypeStruct((6, 2 * (span + D), outs), BF16),
            jax.ShapeDtypeStruct((3, outs, half), BF16),
        ],
        (at_y,),
        (share, other, block, left, right),
        0,
        [sums_at],
    )
    (far_mixed,) = call(
        functools.partial(mixed_kernel, scale),
        [jax.ShapeDtypeStruct((2, 2 * (span + D), outs), BF16)],
        (),
        (weights, *far),
        0,
        [sums_at],
    )
    mixed = [near_mixed, far_mixed]
    near = jnp.concatenate([m[:, : span + D] for m in mixed], axis=0)
    away = jnp.concatenate([m[:, span + D :] for m in mixed], axis=0)
    mate = swap(jnp.where(first, away, near))
    total = jnp.where(first, near, away).astype(F32) + mate.astype(F32)
    edge = jnp.where(first, total[:, :D], total[:, span:]).astype(BF16)
    edge = lax.ppermute(edge, SEQ, outward())
    terms, edge = lax.optimization_barrier((terms, edge))
    edge = edge.astype(F32)
    total = jnp.where(
        first,
        jnp.concatenate([total[:, D : 2 * D] + edge, total[:, 2 * D :]], axis=1),
        jnp.concatenate([total[:, : span - D], total[:, span - D : span] + edge], axis=1),
    )
    total = total.astype(BF16).reshape(4, seqs, span, outs)
    back = [total[0]] + [
        lax.ppermute(total[i], "x", around_x(-d)) for i, d in enumerate(ORDER) if d > 0
    ]

    at = (z * piece, core * half + ylo * quarter)
    own_param = lax.dynamic_slice(kernel.reshape(3 * rows, width), at, (piece, quarter))
    own_noise = lax.dynamic_slice(
        jnp.transpose(noise, (1, 0, 2)).reshape(3 * rows, width), at, (piece, quarter)
    )
    (copies,) = call(
        functools.partial(update_kernel, eta),
        [jax.ShapeDtypeStruct((16, piece, quarter), BF16)],
        (),
        (terms, own_param, own_noise),
        0,
    )
    sent = lax.all_to_all(copies, ("z", "ylo"), 0, 0, tiled=True)

    back, sent = lax.optimization_barrier((back, sent))
    result = jnp.zeros((seqs, span, width), BF16)
    for rows_back, d in zip(back, ORDER):
        result = lax.dynamic_update_slice_in_dim(result, rows_back, lax.rem(x + d, 4) * outs, 2)
    outputs = (inputs.astype(F32) + result.astype(F32)).astype(BF16)

    (sent,) = call(
        place_kernel,
        [jax.ShapeDtypeStruct((3 * rows, width), BF16)],
        (at_core,),
        (sent, swap(sent)),
        0,
    )
    new_param = jnp.transpose(sent.reshape(3, rows, width), (1, 0, 2))
    return (outputs, new_param)


def solution(mesh):
    fine = Mesh(mesh.devices.reshape(8, 2, 2, 4, 2), ("z", "ylo", "core", "x", "yhi"))
    spread = P(("x", "yhi"), SEQ, None)
    placed = (spread, P(), P(("x", "yhi"), None, None), spread, P(("x", "yhi"), None, None))
    return jax.shard_map(
        shards,
        mesh=fine,
        in_specs=placed,
        out_specs=(spread, P(("x", "yhi"), None, None)),
        check_vma=False,
    )
```

```python
import functools
import math

import jax
import jax.numpy as jnp
from jax import lax
from jax.experimental import pallas as pl
from jax.experimental.pallas import tpu as pltpu
from jax.sharding import Mesh, PartitionSpec as P

D = 16
F32, BF16 = jnp.float32, jnp.bfloat16
SEQ = ("z", "ylo", "core")
PLANE = ("ylo", "yhi")


def around_x(step):
    return [(i, (i + step) % 4) for i in range(4)]


def around_y(step):
    at = [(y % 2) * 2 + y // 2 for y in range(4)]
    return [(at[y], at[(y + step) % 4]) for y in range(4)]


def other_y():
    at = [(y % 2) * 2 + y // 2 for y in range(4)]
    return [(at[y], at[3 - y]) for y in range(4)]


def outward():
    n = lax.axis_size(SEQ)
    pairs = []
    for i in range(n):
        j = i - 1 if i % 2 == 0 else i + 1
        if 0 <= j < n:
            pairs.append((i, j))
    return pairs


def swap(v):
    return lax.ppermute(v, "core", [(0, 1), (1, 0)])


def normalise(values, gain):
    floats = values.astype(F32)
    factor = lax.rsqrt(jnp.mean(floats * floats, axis=-1, keepdims=True) + 1e-06)
    return jax.nn.gelu(floats * factor * gain).astype(BF16)


def in_vmem(count):
    return [pl.BlockSpec(memory_space=pltpu.VMEM)] * count


def call(kernel, shapes, scalars, arrays, flops, scratch=()):
    size = sum(math.prod(a.shape) * a.dtype.itemsize for a in (*arrays, *shapes))
    return pl.pallas_call(
        kernel,
        out_shape=shapes,
        in_specs=[pl.BlockSpec(memory_space=pltpu.SMEM)] * len(scalars) + in_vmem(len(arrays)),
        out_specs=in_vmem(len(shapes)),
        scratch_shapes=list(scratch),
        cost_estimate=pl.CostEstimate(flops=flops, bytes_accessed=size, transcendentals=0),
        compiler_params=pltpu.CompilerParams(vmem_limit_bytes=40 * 2**20),
    )(*scalars, *arrays)


ORDER = (0, 1, 3, 2)


def turn_kernel(x, source, *targets):
    n = source.shape[1] - 2 * D
    for k, target in enumerate(targets):
        for i, d in enumerate(ORDER):
            for b in range(2):
                place = ((x[0] - d) & 3) * 2 + b
                at = (2 * i + b) * n
                target[:, at : at + n] = source[place, (2 - k) * D : (2 - k) * D + n].T


def sequences(blocks):
    return [ref.at[b] for ref in blocks for b in range(ref.shape[0])]


def near_grad_kernel(*refs):
    turned, blocks, out = refs[:3], sequences(refs[3:-1]), refs[-1]
    n, width = blocks[0].shape
    tile = 256
    for k in range(3):
        for at in range(0, width, tile):
            total = jnp.zeros((out.shape[1], tile), F32)
            for b, block in enumerate(blocks):
                total += jnp.dot(
                    turned[k][:, b * n : (b + 1) * n],
                    block[:, at : at + tile],
                    preferred_element_type=F32,
                )
            out[k, :, at : at + tile] = total


def grad_kernel(scale, over, sums, *refs):
    turned, blocks, out = refs[:3], sequences(refs[3:-1]), refs[-1]
    outs = turned[0].shape[0]
    rows = outs // 2
    n, width = blocks[0].shape
    quarter, tile = width // 2, 256
    seen = turned[0].shape[1] - len(blocks) * n
    for k in range(3):
        for at in range(0, width, tile):
            total = sums[k, :, at : at + tile]
            for b, block in enumerate(blocks):
                total += jnp.dot(
                    turned[k][:, seen + b * n : seen + (b + 1) * n],
                    block[:, at : at + tile],
                    preferred_element_type=F32,
                )
            total = (total * scale).astype(BF16)
            for sub in range(2):
                lo, hi = max(at, sub * quarter), min(at + tile, (sub + 1) * quarter)
                if lo >= hi:
                    continue
                for part in range(2):
                    slot = (2 * part + sub - over[0] + 4) & 3
                    out[slot, k * rows : (k + 1) * rows, lo - sub * quarter : hi - sub * quarter] = (
                        total[part * rows : (part + 1) * rows, lo - at : hi - at]
                    )


def update_kernel(eta, terms, param, noise, out):
    total = jnp.sum(terms[...].astype(F32), axis=0)
    new = (
        param[...].astype(F32) - eta * total + math.sqrt(2.0 * eta) * noise[...].astype(F32)
    ).astype(BF16)
    for i in range(out.shape[0]):
        out[i] = new


def place_kernel(core, own, mate, out):
    rows, columns = own.shape[1:]
    for source, side in ((own, core[0]), (mate, 1 - core[0])):
        for i in range(own.shape[0]):
            start = pl.multiple_of(side * (2 * columns) + (i % 2) * columns, columns)
            out[(i // 2) * rows : (i // 2 + 1) * rows, pl.ds(start, columns)] = source[i]


def mixed_kernel(scale, over, one, two, *refs):
    blocks, (result, weights, total) = sequences(refs[:-3]), refs[-3:]
    rows, n = one.shape[1], blocks[0].shape[0]
    swapped = jnp.where(over[0] < 2, 0, rows)
    for k in range(3):
        weights[k, pl.ds(pl.multiple_of(swapped, rows), rows), :] = one[k]
        weights[k, pl.ds(pl.multiple_of(rows - swapped, rows), rows), :] = two[k]
    for b, block in enumerate(blocks):
        for k in (0, 2, 1):
            part = lax.dot_general(
                block[...], weights[k], (((1,), (1,)), ((), ())), preferred_element_type=F32
            )
            if k == 0:
                total[2 * D :] = part
            elif k == 2:
                total[: 2 * D] = part[: 2 * D]
                total[2 * D : n] += part[2 * D :]
            else:
                total[D : D + n] += part
        result[b] = (total[...] * scale).astype(BF16)


def shards(inputs, gain, param, cotangent, noise):
    seqs, span, width = inputs.shape
    rows = param.shape[0]
    outs = 2 * rows
    half = width // 2
    quarter = half // 2
    piece = 3 * rows // 8
    scale = 1.0 / math.sqrt(3.0 * width)
    total_rows = seqs * span * 256
    eta = math.sqrt(3.0 * width / total_rows)
    core, ylo, yhi, x, z = (lax.axis_index(a) for a in ("core", "ylo", "yhi", "x", "z"))
    y = 2 * yhi + ylo
    first = core == 0
    at_x = x.astype(jnp.int32).reshape(1)
    at_y = y.astype(jnp.int32).reshape(1)

    edge = jnp.where(first, cotangent[:, :D], cotangent[:, span - D :])
    values, edge = lax.optimization_barrier((inputs, edge))
    edge = lax.ppermute(edge, SEQ, outward())
    cot = jnp.where(
        first,
        jnp.concatenate([edge, cotangent], axis=1),
        jnp.concatenate([cotangent, edge], axis=1),
    )
    cot = jnp.transpose(cot.reshape(seqs, span + D, 4, outs), (2, 0, 1, 3))
    cot = lax.all_to_all(cot.reshape(8, span + D, outs), "x", 0, 0, tiled=True)

    own = normalise(values, gain)
    low, high = own[:, :, :half], own[:, :, half:]
    mine = jnp.where(first, low, high)
    mate = swap(jnp.where(first, high, low))
    block = jnp.concatenate([jnp.where(first, mine, mate), jnp.where(first, mate, mine)], axis=1)
    left = lax.ppermute(block, "x", around_x(1))
    right = lax.ppermute(block, "x", around_x(-1))
    far = [lax.ppermute(left[:1], "x", around_x(1)), lax.ppermute(right[1:], "x", around_x(-1))]
    kernel = jnp.transpose(param, (1, 0, 2))
    block, kernel = lax.optimization_barrier((block, kernel))
    share = lax.dynamic_slice_in_dim(kernel, core * half, half, 2)
    other = lax.ppermute(share, PLANE, other_y())

    cot, other, left, right = lax.optimization_barrier((cot, other, left, right))
    mate = swap(cot)
    cot = jnp.concatenate([jnp.where(first, cot, mate), jnp.where(first, mate, cot)], axis=1)
    turned = call(
        turn_kernel, [jax.ShapeDtypeStruct((outs, 8 * 2 * span), BF16)] * 3, (at_x,), (cot,), 0
    )

    work = 2 * 2 * span * outs * half * 3
    (sums,) = call(
        near_grad_kernel,
        [jax.ShapeDtypeStruct((3, outs, half), F32)],
        (),
        (*turned, block, left, right),
        6 * work,
    )
    far, sums = lax.optimization_barrier((far, sums))
    (grad,) = call(
        functools.partial(grad_kernel, scale),
        [jax.ShapeDtypeStruct((4, 3 * rows, quarter), BF16)],
        (at_y,),
        (sums, *turned, *far),
        2 * work,
    )
    terms = [grad[0]] + [lax.ppermute(grad[d], PLANE, around_y(d)) for d in range(1, 4)]
    summed = sum(t.astype(F32) for t in terms).astype(BF16)

    summed, far = lax.optimization_barrier((summed, far))
    terms = lax.all_to_all(summed.reshape(8, piece, quarter), "z", 0, 0, tiled=True)

    mixed = []
    for group in ((block, left, right), far):
        (part,) = call(
            functools.partial(mixed_kernel, scale),
            [jax.ShapeDtypeStruct((sum(g.shape[0] for g in group), 2 * (span + D), outs), BF16)],
            (at_y,),
            (share, other, *group),
            0,
            [pltpu.VMEM((3, outs, half), BF16), pltpu.VMEM((2 * (span + D), outs), F32)],
        )
        mixed.append(part)
    near = jnp.concatenate([m[:, : span + D] for m in mixed], axis=0)
    away = jnp.concatenate([m[:, span + D :] for m in mixed], axis=0)
    mate = swap(jnp.where(first, away, near))
    total = jnp.where(first, near, away).astype(F32) + mate.astype(F32)
    edge = jnp.where(first, total[:, :D], total[:, span:]).astype(BF16)
    edge = lax.ppermute(edge, SEQ, outward())
    terms, edge = lax.optimization_barrier((terms, edge))
    edge = edge.astype(F32)
    total = jnp.where(
        first,
        jnp.concatenate([total[:, D : 2 * D] + edge, total[:, 2 * D :]], axis=1),
        jnp.concatenate([total[:, : span - D], total[:, span - D : span] + edge], axis=1),
    )
    total = total.astype(BF16).reshape(4, seqs, span, outs)
    back = [total[0]] + [
        lax.ppermute(total[i], "x", around_x(-d)) for i, d in enumerate(ORDER) if d > 0
    ]

    at = (z * piece, core * half + ylo * quarter)
    own_param = lax.dynamic_slice(kernel.reshape(3 * rows, width), at, (piece, quarter))
    own_noise = lax.dynamic_slice(
        jnp.transpose(noise, (1, 0, 2)).reshape(3 * rows, width), at, (piece, quarter)
    )
    (copies,) = call(
        functools.partial(update_kernel, eta),
        [jax.ShapeDtypeStruct((16, piece, quarter), BF16)],
        (),
        (terms, own_param, own_noise),
        0,
    )
    sent = lax.all_to_all(copies, ("z", "ylo"), 0, 0, tiled=True)

    back, sent = lax.optimization_barrier((back, sent))
    result = jnp.zeros((seqs, span, width), BF16)
    for rows_back, d in zip(back, ORDER):
        result = lax.dynamic_update_slice_in_dim(result, rows_back, lax.rem(x + d, 4) * outs, 2)
    outputs = (inputs.astype(F32) + result.astype(F32)).astype(BF16)

    (sent,) = call(
        place_kernel,
        [jax.ShapeDtypeStruct((3 * rows, width), BF16)],
        (core.astype(jnp.int32).reshape(1),),
        (sent, swap(sent)),
        0,
    )
    new_param = jnp.transpose(sent.reshape(3, rows, width), (1, 0, 2))
    return (outputs, new_param)


def solution(mesh):
    fine = Mesh(mesh.devices.reshape(8, 2, 2, 4, 2), ("z", "ylo", "core", "x", "yhi"))
    spread = P(("x", "yhi"), SEQ, None)
    placed = (spread, P(), P(("x", "yhi"), None, None), spread, P(("x", "yhi"), None, None))
    return jax.shard_map(
        shards,
        mesh=fine,
        in_specs=placed,
        out_specs=(spread, P(("x", "yhi"), None, None)),
        check_vma=False,
    )
```
